128 devices in a mesh: seq: 64 (over z, x, y_hi, core), ch: 2 (over y_lo).
Axes of the slice: x: 4, y: 4 (y_hi: 2, y_lo: 2; y = y_hi * 2 + y_lo), z: 4, core: 2. Of those that a mesh axis runs over, the one named last changes fastest.
Arguments:
- inputs: bfloat16 [2, 65536, 1536], P(None, 'seq', 'ch'), may hold values from -6 to 6
- cotangent: bfloat16 [2, 65536, 1536], P(None, 'seq', 'ch'), may hold values from -6 to 6
- conv_out: bfloat16 [2, 65536, 768], P(None, 'seq'), may hold values from -6 to 6
- conv_weight: bfloat16 [3, 1536, 768], P(None, 'ch'), may hold values from -0.09375 to 0.09375
- proj_weight: bfloat16 [768, 1536], P(None, 'ch'), may hold values from -0.21875 to 0.21875
Outputs:
- grad_inputs: bfloat16 [2, 65536, 1536], P(None, 'seq', 'ch')
- grad_conv: bfloat16 [3, 1536, 768], P(None, 'ch')
- grad_proj: bfloat16 [768, 1536], P(None, 'ch')
The draws below stay inside these ranges and needn't reach their ends.
All inputs are finite; a program needn't handle non-finite values.
Results may differ from the reference program's by a relative error of at most 0.0061.
Values may be sent and summed in bfloat16 or wider, within the bound.
A program may use at most 128 MiB of HBM per device.

```python
import math
import jax
import jax.numpy as jnp
from jax import lax

C = 1536
F = 768
DILATION_STEP = 2048
B = 2
SEQUENCE_LENGTH = 65536


def level_of(stream_key, shape, pieces, low, top_value):
    def one(dim, blocks):
        steps = jax.random.uniform(jax.random.fold_in(jax.random.fold_in(stream_key, 6), dim), (blocks,), jnp.float32, low / len(pieces), top_value / len(pieces))
        return jnp.repeat(jnp.exp(steps), shape[dim] // blocks).reshape((-1,) + (1,) * (len(shape) - dim - 1))

    level = one(*pieces[0])
    for cut in pieces[1:]:
        level = level * one(*cut)
    return level


def gaussian(key, dims, scale, reach, cuts=(), dtype=jnp.bfloat16):
    array = jax.random.normal(key, dims, jnp.float32) * scale
    if len(cuts) > 0:
        array = level_of(key, dims, cuts, -0.22, 0.18) * array
    return jnp.clip(array, min=-reach, max=reach).astype(dtype)


def setup_inputs(seed: int = 0) -> dict:
    key_list = jax.random.split(jax.random.key(seed), 6)
    inputs = gaussian(key_list[0], (B, SEQUENCE_LENGTH, C), 1.0, 6.0, ((1, 64), (2, 2)))
    cotangent = gaussian(key_list[1], (B, SEQUENCE_LENGTH, C), 1.0, 6.0, ((1, 64), (2, 2)))
    conv_out = gaussian(key_list[2], (B, SEQUENCE_LENGTH, F), 1.0, 6.0, ((1, 64),))
    conv_weight = gaussian(key_list[3], (3, C, F), (3 * C) ** -0.5, 0.09375, ((1, 2),))
    proj_weight = gaussian(key_list[4], (F, C), F ** -0.5, 0.21875, ((1, 2),))
    return dict(inputs=inputs, cotangent=cotangent, conv_out=conv_out, conv_weight=conv_weight, proj_weight=proj_weight)


def contract_rows(left, right):
    return lax.dot_general(left, right, (((0,), (0,)), ((), ())), preferred_element_type=jnp.float32)

def gelu_parts(values):
    wide = values.astype(jnp.float32)
    cumul = 0.5 * (1.0 + jax.scipy.special.erf(wide / math.sqrt(2.0)))
    dense = jnp.exp(-0.5 * wide * wide) / math.sqrt(2.0 * math.pi)
    return (wide * cumul, cumul + wide * dense)

def reference(inputs, cotangent, conv_out, conv_weight, proj_weight):
    row_count = B * SEQUENCE_LENGTH
    flat_g = cotangent.reshape(row_count, C)
    middle_gradient = jnp.dot(flat_g, proj_weight.T, preferred_element_type=jnp.float32).astype(jnp.bfloat16)
    middle_gradient = middle_gradient.reshape(B, SEQUENCE_LENGTH, F)
    following = jnp.pad(middle_gradient[:, DILATION_STEP:], ((0, 0), (0, DILATION_STEP), (0, 0)))
    preceding = jnp.pad(middle_gradient[:, :SEQUENCE_LENGTH - DILATION_STEP], ((0, 0), (DILATION_STEP, 0), (0, 0)))
    tap_list = (following.reshape(row_count, F), middle_gradient.reshape(row_count, F), preceding.reshape(row_count, F))
    grad_hidden = jnp.zeros((row_count, C), jnp.float32)
    for tap_index in range(3):
        grad_hidden = grad_hidden + jnp.dot(tap_list[tap_index], conv_weight[tap_index].T, preferred_element_type=jnp.float32)
    hidden_full, deriv = gelu_parts(inputs.reshape(row_count, C))
    hidden = hidden_full.astype(jnp.bfloat16)
    grad_inputs = (flat_g.astype(jnp.float32) + grad_hidden * deriv).astype(jnp.bfloat16).reshape(B, SEQUENCE_LENGTH, C)
    grad_scale = 1.0 / math.sqrt(float(row_count))
    grad_conv = jnp.stack([contract_rows(hidden, tap_list[tap_index]) * grad_scale for tap_index in range(3)])
    grad_proj = contract_rows(conv_out.reshape(row_count, F), flat_g) * grad_scale
    return (grad_inputs, grad_conv.astype(jnp.bfloat16), grad_proj.astype(jnp.bfloat16))
```

```python
import functools
import math

import jax
import jax.numpy as jnp
from jax import lax
from jax.experimental import pallas as pl
from jax.experimental.pallas import tpu as pltpu
from jax.sharding import PartitionSpec as P

MESH = pl.DeviceIdType.MESH
ROWS = 2048
CH = 768
FULL = 768
FW = 256
NF = FULL // FW
RB = 256
NB = ROWS // RB
NT = NF * NB
WINDOW = 6
LAG = 2
SLAB = 3 * CH
ZP = SLAB // 4
XP = ZP // 8
SCALE = 1.0 / math.sqrt(131072.0)
BF = jnp.bfloat16
F32 = jnp.float32


def dot(a, b):
    return lax.dot_general(a, b, (((1,), (0,)), ((), ())), preferred_element_type=F32)


def dot_t(a, b):
    return lax.dot_general(a, b, (((1,), (1,)), ((), ())), preferred_element_type=F32)


def wait_for(ref, sem):
    pltpu.make_async_copy(ref, ref, sem).wait()


def kernel(
    inp_h, cot_h, cout_h, cw_h, pw_h, gi_h, wg_h,
    cot, io, h_t, der, pw, cw, part, mid, mid_q, mid_x, gh,
    slab, own32, z32, cs, cr, zs, zr, xs, xr, fin,
    ld_sem, out_sem, wout_sem,
    e_send, e_recv, q_send, q_recv, x_send, x_recv,
    c_send, c_recv, zz_send, zz_recv, xy_send, xy_recv,
    axy_send, axy_recv, az_send, az_recv, ac_send, ac_recv,
):
    s = lax.axis_index("seq")
    c = lax.axis_index("ch")
    core = s % 2
    yh = (s // 2) % 2
    p = (s // 2) % 8
    z = s // 16

    def dev(seq, ch):
        return {"seq": seq, "ch": ch}

    partner = dev(s, 1 - c)
    across = dev(s + 2 - 4 * yh, 1 - c)
    ahead = s + 4 - 8 * yh
    behind = s - 4 + 8 * yh
    has_dst = jnp.logical_and(ahead >= 0, ahead < 64)
    has_src = jnp.logical_and(behind >= 0, behind < 64)
    twin = dev(s + 1 - 2 * core, c)

    def z_peer(d):
        return (z + d) % 4

    def z_dev(d):
        return dev(z_peer(d) * 16 + s % 16, c)

    def p_peer(d):
        return (p + d) % 8

    def p_dev(d):
        return dev(z * 16 + p_peer(d) * 2 + core, c)

    ld_cot = pltpu.make_async_copy(cot_h, cot, ld_sem.at[0])
    ld_pw = pltpu.make_async_copy(pw_h, pw, ld_sem.at[1])
    ld_cout = pltpu.make_async_copy(cout_h, io, ld_sem.at[2])
    ld_inp = pltpu.make_async_copy(inp_h, io, ld_sem.at[3])
    ld_cw = [
        pltpu.make_async_copy(cw_h.at[:, :, pl.ds(f * FW, FW)], cw.at[f], ld_sem.at[4 + f])
        for f in range(NF)
    ]
    ld_cot.start()
    ld_pw.start()
    ld_cout.start()
    for cp in ld_cw:
        cp.start()

    barrier = pltpu.get_barrier_semaphore()

    def greet(device):
        pl.semaphore_signal(barrier, inc=1, device_id=device, device_id_type=MESH)

    greet(partner)
    greet(across)
    greet(twin)
    for d in range(1, 4):
        greet(z_dev(d))
    for d in range(1, 8):
        greet(p_dev(d))

    far_dst = jnp.logical_and(has_dst, ahead // 16 != z)
    far_src = jnp.logical_and(has_src, behind // 16 != z)

    @pl.when(far_dst)
    def _():
        greet(dev(ahead, c))

    @pl.when(far_src)
    def _():
        greet(dev(behind, c))

    pl.semaphore_wait(barrier, 13 + far_dst.astype(jnp.int32) + far_src.astype(jnp.int32))

    def block(ref, t):
        return ref.at[t // NB, pl.ds(pl.multiple_of((t % NB) * RB, RB), RB)]

    def start_e(t):
        pltpu.make_async_remote_copy(
            src_ref=block(part, t), dst_ref=block(mid, t), send_sem=e_send, recv_sem=e_recv.at[t],
            device_id=partner, device_id_type=MESH,
        ).start()

    def start_q(t):
        pltpu.make_async_remote_copy(
            src_ref=block(mid, t), dst_ref=block(mid_q, t), send_sem=q_send, recv_sem=q_recv.at[t],
            device_id=across, device_id_type=MESH,
        ).start()

    def forward_x(t):
        wait_for(block(mid_q, t), q_recv.at[t])

        @pl.when(has_dst)
        def _():
            pltpu.make_async_remote_copy(
                src_ref=block(mid_q, t), dst_ref=block(mid_x, t), send_sem=x_send, recv_sem=x_recv.at[t // NB],
                device_id=dev(ahead, c), device_id_type=MESH,
            ).start()

    ld_cot.wait()
    ld_pw.wait()

    def part_chunk(f, _):
        weights = pw[pl.ds(pl.multiple_of(f * FW, FW), FW), :]

        def part_block(r, _):
            rows = pl.ds(pl.multiple_of(r * RB, RB), RB)
            part[f, rows, :] = dot_t(cot[rows, :], weights).astype(BF)
            t = f * NB + r

            @pl.when(t < WINDOW)
            def _():
                start_e(t)

            return 0

        return lax.fori_loop(0, NB, part_block, 0)

    lax.fori_loop(0, NF, part_chunk, 0)

    @pl.when(jnp.logical_not(has_src))
    def _():
        def clear(i, _):
            mid_x[i // 32, pl.ds(pl.multiple_of((i % 32) * 64, 64), 64), :] = jnp.zeros((64, FW), BF)
            return 0

        lax.fori_loop(0, 32 * NF, clear, 0)

    def service(t):
        wait_for(block(mid, t), e_recv.at[t])
        nxt = t + WINDOW

        @pl.when(nxt < NT)
        def _():
            start_e(nxt)

        f, r0 = t // NB, (t % NB) * RB

        def add(i, _):
            rows = pl.ds(pl.multiple_of(r0 + i * 64, 64), 64)
            mid[f, rows, :] = (part[f, rows, :].astype(F32) + mid[f, rows, :].astype(F32)).astype(BF)
            return 0

        lax.fori_loop(0, RB // 64, add, 0)
        start_q(t)

    def store_slab(row, value):
        rows = pl.ds(pl.multiple_of(row, 256), 256)
        slab[0, rows, :] = value[:, :128]
        slab[1, rows, :] = value[:, 128:]

    ld_cout.wait()

    def turn(i, _):
        span = pl.ds(pl.multiple_of(i * 128, 128), 128)
        h_t[:, span] = io[span, :].T
        return 0

    lax.fori_loop(0, ROWS // 128, turn, 0)
    ld_inp.start()
    for k in range(3):
        def proj_tile(i, _, k=k):
            rows = pl.ds(pl.multiple_of(i * 256, 256), 256)
            store_slab(k * CH + i * 256, dot(h_t[rows, :], cot[:, k * 256:(k + 1) * 256]))
            return 0

        lax.fori_loop(0, 3, proj_tile, 0)

    def core_send(g):
        def cast(i, _):
            rows = pl.ds(pl.multiple_of(i * 64, 64), 64)
            cs[g, rows, :] = slab[1 - core, rows, :].astype(BF)
            return 0

        lax.fori_loop(0, SLAB // 64, cast, 0)
        pltpu.make_async_remote_copy(
            src_ref=cs.at[g], dst_ref=cr.at[g], send_sem=c_send, recv_sem=c_recv.at[g],
            device_id=twin, device_id_type=MESH,
        ).start()

    def z_send(g):
        wait_for(cr.at[g], c_recv.at[g])

        def add(i, _):
            rows = pl.ds(pl.multiple_of(i * 64, 64), 64)
            total = slab[core, rows, :] + cr[g, rows, :].astype(F32)
            slab[core, rows, :] = total
            zs[g, i // (ZP // 64), pl.ds(pl.multiple_of((i % (ZP // 64)) * 64, 64), 64), :] = total.astype(BF)
            return 0

        lax.fori_loop(0, SLAB // 64, add, 0)
        own32[...] = slab[core, pl.ds(pl.multiple_of(z * ZP, 64), ZP), :]
        for d in range(1, 4):
            pltpu.make_async_remote_copy(
                src_ref=zs.at[g, z_peer(d)], dst_ref=zr.at[g, d - 1], send_sem=zz_send, recv_sem=zz_recv.at[g],
                device_id=z_dev(d), device_id_type=MESH,
            ).start()

    def x_send_sum(g):
        wait_for(zr.at[g], zz_recv.at[g])

        def add(i, _):
            rows = pl.ds(pl.multiple_of(i * 64, 64), 64)
            z32[rows, :] = (own32[rows, :] + zr[g, 0, rows, :].astype(F32)) + (
                zr[g, 1, rows, :].astype(F32) + zr[g, 2, rows, :].astype(F32)
            )
            return 0

        lax.fori_loop(0, ZP // 64, add, 0)
        for i in range(8):
            xs[g, i] = z32[i * XP:(i + 1) * XP, :].astype(BF)
        for d in range(1, 8):
            pltpu.make_async_remote_copy(
                src_ref=xs.at[g, p_peer(d)], dst_ref=xr.at[g, d - 1], send_sem=xy_send, recv_sem=xy_recv.at[g],
                device_id=p_dev(d), device_id_type=MESH,
            ).start()

    def finish(g):
        wait_for(xr.at[g], xy_recv.at[g])
        total = z32[pl.ds(pl.multiple_of(p * XP, 8), XP), :]
        for d in range(7):
            total = total + xr[g, d].astype(F32)
        fin[g, core, z, p] = (total * SCALE).astype(BF)
        for d in range(1, 8):
            piece = fin.at[g, core, z, p]
            pltpu.make_async_remote_copy(
                src_ref=piece, dst_ref=piece, send_sem=axy_send, recv_sem=axy_recv.at[g],
                device_id=p_dev(d), device_id_type=MESH,
            ).start()

    def gather_z(g):
        wait_for(xr.at[g], axy_recv.at[g])
        for d in range(1, 4):
            piece = fin.at[g, core, z]
            pltpu.make_async_remote_copy(
                src_ref=piece, dst_ref=piece, send_sem=az_send, recv_sem=az_recv.at[g],
                device_id=z_dev(d), device_id_type=MESH,
            ).start()

    def gather_core(g):
        wait_for(fin.at[g, core, pl.ds(0, 3)], az_recv.at[g])
        piece = fin.at[g, core]
        pltpu.make_async_remote_copy(
            src_ref=piece, dst_ref=piece, send_sem=ac_send, recv_sem=ac_recv.at[g],
            device_id=twin, device_id_type=MESH,
        ).start()

    def write_out(g):
        wait_for(fin.at[g, 1 - core], ac_recv.at[g])
        pltpu.make_async_copy(fin.at[g], wg_h.at[g], wout_sem).start()

    core_send(0)

    def gelu(i):
        def tile(j, _):
            rows = pl.ds(pl.multiple_of(i * RB + j * 128, 128), 128)

            def strip(m, _):
                sub = pl.ds(pl.multiple_of(i * RB + j * 128 + m * 16, 16), 16)
                wide = io[sub, :].astype(F32)
                cumul = 0.5 * (1.0 + lax.erf(wide * (1.0 / math.sqrt(2.0))))
                dense = jnp.exp(-0.5 * wide * wide) * (1.0 / math.sqrt(2.0 * math.pi))
                der[sub, :] = cumul + wide * dense
                io[sub, :] = (wide * cumul).astype(BF)
                return 0

            lax.fori_loop(0, 8, strip, 0)
            h_t[:, rows] = io[rows, :].T
            return 0

        lax.fori_loop(0, RB // 128, tile, 0)

    ld_inp.wait()
    for i in range(NB):
        service(i)
        if i >= LAG:
            forward_x(i - LAG)
        if i == 2:
            z_send(0)
        if i == 4:
            x_send_sum(0)
        if i == 6:
            finish(0)
        gelu(i)

    for cp in ld_cw:
        cp.wait()

    tap_q = 2 * yh
    tap_x = 2 - 2 * yh

    def weight_tap(f, tap, taps):
        def tile(i, _):
            rows = pl.ds(pl.multiple_of(i * 256, 256), 256)
            store_slab(tap * CH + i * 256, dot(h_t[rows, :], taps[f]))
            return 0

        lax.fori_loop(0, CH // 256, tile, 0)

    def data_rows(g, first, count):
        f = g - 1

        def tile(i, _):
            rows = pl.ds(pl.multiple_of(i * RB, RB), RB)
            total = dot_t(mid[f, rows, :], cw[f, 1])
            total = total + dot_t(mid_q[f, rows, :], cw[f, tap_q])
            total = total + dot_t(mid_x[f, rows, :], cw[f, tap_x])

            @pl.when(g == 1)
            def _():
                gh[rows, :] = total

            @pl.when(g > 1)
            def _():
                gh[rows, :] = gh[rows, :] + total

            @pl.when(g == NF)
            def _():
                def strip(m, _):
                    sub = pl.ds(pl.multiple_of(i * RB + m * 16, 16), 16)
                    io[sub, :] = (cot[sub, :].astype(F32) + gh[sub, :] * der[sub, :]).astype(BF)
                    return 0

                lax.fori_loop(0, RB // 16, strip, 0)
                pltpu.make_async_copy(io.at[rows], gi_h.at[rows], out_sem).start()

            return 0

        lax.fori_loop(first, first + count, tile, 0)

    def phase(g, _):
        f = g - 1

        def serve(i):
            t = g * NB + i

            @pl.when(g < NF)
            def _():
                service(t)

            if i < LAG:
                forward_x(t - LAG)
            else:
                @pl.when(g < NF)
                def _():
                    forward_x(t - LAG)

        serve(0)
        gather_z(g - 1)
        weight_tap(f, 1, mid)
        serve(1)
        weight_tap(f, tap_q, mid_q)
        serve(2)
        gather_core(g - 1)
        serve(3)

        @pl.when(has_src)
        def _():
            wait_for(mid_x.at[f], x_recv.at[f])

        weight_tap(f, tap_x, mid_x)
        core_send(g)
        serve(4)
        data_rows(g, 0, NB // 2)
        serve(5)
        z_send(g)
        write_out(g - 1)
        data_rows(g, NB // 2, NB // 4)
        serve(6)
        x_send_sum(g)
        data_rows(g, NB // 2 + NB // 4, NB // 4)
        serve(7)
        finish(g)
        return 0

    lax.fori_loop(1, NF + 1, phase, 0)
    gather_z(NF)
    gather_core(NF)
    write_out(NF)

    wait_for(part, e_send)
    wait_for(mid, q_send)

    @pl.when(has_dst)
    def _():
        wait_for(mid_q, x_send)

    wait_for(cs, c_send)
    wait_for(zr, zz_send)
    wait_for(xr, xy_send)
    wait_for(xr, axy_send)
    for g in range(NF + 1):
        wait_for(fin.at[g, 0, pl.ds(0, 3)], az_send)
        wait_for(fin.at[g, 0], ac_send)
    wait_for(io, out_sem)
    wait_for(fin, wout_sem)


def shards(inputs, cotangent, conv_out, conv_weight, proj_weight):
    any_spec = pl.BlockSpec(memory_space=pl.ANY)
    dma = pltpu.SemaphoreType.DMA
    slabs = NF + 1
    rows_bf = pltpu.VMEM((ROWS, CH), BF)
    chunks = pltpu.VMEM((NF, ROWS, FW), BF)
    flat = [a.reshape(ROWS, CH) for a in (inputs, cotangent, conv_out)]
    grad_inputs, raw = pl.pallas_call(
        kernel,
        out_shape=(
            jax.ShapeDtypeStruct((ROWS, CH), BF),
            jax.ShapeDtypeStruct((slabs, 2, 4, 8, XP, 128), BF),
        ),
        in_specs=[any_spec] * 5,
        out_specs=(any_spec, any_spec),
        scratch_shapes=[
            rows_bf, rows_bf, pltpu.VMEM((CH, ROWS), BF), pltpu.VMEM((ROWS, CH), F32),
            pltpu.VMEM((FULL, CH), BF), pltpu.VMEM((NF, 3, CH, FW), BF),
            chunks, chunks, chunks, chunks, pltpu.VMEM((ROWS, CH), F32),
            pltpu.VMEM((2, SLAB, 128), F32), pltpu.VMEM((ZP, 128), F32), pltpu.VMEM((ZP, 128), F32),
            pltpu.VMEM((slabs, SLAB, 128), BF), pltpu.VMEM((slabs, SLAB, 128), BF),
            pltpu.VMEM((slabs, 4, ZP, 128), BF), pltpu.VMEM((slabs, 3, ZP, 128), BF),
            pltpu.VMEM((slabs, 8, XP, 128), BF), pltpu.VMEM((slabs, 7, XP, 128), BF),
            pltpu.VMEM((slabs, 2, 4, 8, XP, 128), BF),
            dma((4 + NF,)), dma, dma,
            dma, dma((NT,)), dma, dma((NT,)), dma, dma((NF,)),
        ] + [dma, dma((slabs,))] * 6,
        compiler_params=pltpu.CompilerParams(
            collective_id=0, has_side_effects=True, vmem_limit_bytes=62 * 1024 * 1024
        ),
    )(*flat, conv_weight, proj_weight)
    raw = raw.reshape(slabs, 2, 3, CH, 128)
    grad_proj = raw[0].transpose(2, 1, 0, 3).reshape(FULL, CH)
    grad_conv = raw[1:].transpose(2, 3, 0, 1, 4).reshape(3, CH, FULL)
    return (grad_inputs.reshape(inputs.shape), grad_conv, grad_proj)


def solution(mesh):
    in_specs = (
        P(None, "seq", "ch"),
        P(None, "seq", "ch"),
        P(None, "seq", None),
        P(None, "ch", None),
        P(None, "ch"),
    )
    out_specs = (P(None, "seq", "ch"), P(None, "ch", None), P(None, "ch"))
    return jax.shard_map(shards, mesh=mesh, in_specs=in_specs, out_specs=out_specs, check_vma=False)
```

```python
import functools
import math

import jax
import jax.numpy as jnp
from jax import lax
from jax.experimental import pallas as pl
from jax.experimental.pallas import tpu as pltpu
from jax.sharding import PartitionSpec as P

MESH = pl.DeviceIdType.MESH
ROWS = 2048
CH = 768
FULL = 768
FW = 256
NF = FULL // FW
RB = 256
NB = ROWS // RB
NT = NF * NB
WINDOW = 6
LAG = 2
SLAB = 3 * CH
ZH = SLAB // 2
ZP = SLAB // 4
XP = ZP // 8
XS = XP // 3
SCALE = 1.0 / math.sqrt(131072.0)
BF = jnp.bfloat16
F32 = jnp.float32


def dot(a, b):
    return lax.dot_general(a, b, (((1,), (0,)), ((), ())), preferred_element_type=F32)


def dot_t(a, b):
    return lax.dot_general(a, b, (((1,), (1,)), ((), ())), preferred_element_type=F32)


def wait_for(ref, sem):
    pltpu.make_async_copy(ref, ref, sem).wait()


def kernel(
    inp_h, cot_h, cout_h, cw_h, pw_h, gi_h, gc_h, gp_h,
    cot, io, h_t, der, pw, cw, part, mid, mid_q, mid_x, gh,
    slab, z32, cs, cr, as_, ar, bs, br, xs, xr, fin,
    ld_sem, out_sem, wout_sem,
    e_send, e_recv, q_send, q_recv, x_send, x_recv,
    c_send, c_recv, a_send, a_recv, b_send, b_recv, xy_send, xy_recv,
    gx_send, gx_recv, gb_send, gb_recv, ga_send, ga_recv, gc_send, gc_recv,
):
    s = lax.axis_index("seq")
    c = lax.axis_index("ch")
    core = s % 2
    yh = (s // 2) % 2
    p = (s // 2) % 8
    z = s // 16

    def dev(seq, ch):
        return {"seq": seq, "ch": ch}

    partner = dev(s, 1 - c)
    across = dev(s + 2 - 4 * yh, 1 - c)
    ahead = s + 4 - 8 * yh
    behind = s - 4 + 8 * yh
    has_dst = jnp.logical_and(ahead >= 0, ahead < 64)
    has_src = jnp.logical_and(behind >= 0, behind < 64)
    twin = dev(s + 1 - 2 * core, c)

    next_z, mirror_z = z + 1 - 2 * (z % 2), 3 - z
    dev_a = dev((next_z + core * (mirror_z - next_z)) * 16 + s % 16, c)
    dev_b = dev((mirror_z + core * (next_z - mirror_z)) * 16 + s % 16, c)
    upper, middle = z // 2, ((z + 1) // 2) % 2
    half = middle + core * (upper - middle)
    quarter = 2 * half + upper + core * (z % 2 - upper)
    other_quarter = 4 * half + 1 - quarter

    def p_peer(d):
        return (p + d) % 8

    def p_dev(d):
        return dev(z * 16 + p_peer(d) * 2 + core, c)

    ld_cot = pltpu.make_async_copy(cot_h, cot, ld_sem.at[0])
    ld_pw = pltpu.make_async_copy(pw_h, pw, ld_sem.at[1])
    ld_cout = pltpu.make_async_copy(cout_h, io, ld_sem.at[2])
    ld_inp = pltpu.make_async_copy(inp_h, io, ld_sem.at[3])
    ld_cw = [
        pltpu.make_async_copy(cw_h.at[:, :, pl.ds(f * FW, FW)], cw.at[f], ld_sem.at[4 + f])
        for f in range(NF)
    ]
    ld_cot.start()
    ld_pw.start()
    ld_cout.start()
    for cp in ld_cw:
        cp.start()

    barrier = pltpu.get_barrier_semaphore()

    def greet(device):
        pl.semaphore_signal(barrier, inc=1, device_id=device, device_id_type=MESH)

    greet(partner)
    greet(across)
    greet(twin)
    greet(dev_a)
    greet(dev_b)
    for d in range(1, 8):
        greet(p_dev(d))

    far_dst = jnp.logical_and(has_dst, ahead // 16 != z)
    far_src = jnp.logical_and(has_src, behind // 16 != z)

    @pl.when(far_dst)
    def _():
        greet(dev(ahead, c))

    @pl.when(far_src)
    def _():
        greet(dev(behind, c))

    pl.semaphore_wait(barrier, 12 + far_dst.astype(jnp.int32) + far_src.astype(jnp.int32))

    def block(ref, t):
        return ref.at[t // NB, pl.ds(pl.multiple_of((t % NB) * RB, RB), RB)]

    def start_e(t):
        pltpu.make_async_remote_copy(
            src_ref=block(part, t), dst_ref=block(mid, t), send_sem=e_send, recv_sem=e_recv.at[t],
            device_id=partner, device_id_type=MESH,
        ).start()

    def start_q(t):
        pltpu.make_async_remote_copy(
            src_ref=block(mid, t), dst_ref=block(mid_q, t), send_sem=q_send, recv_sem=q_recv.at[t],
            device_id=across, device_id_type=MESH,
        ).start()

    def forward_x(t):
        wait_for(block(mid_q, t), q_recv.at[t])

        @pl.when(has_dst)
        def _():
            pltpu.make_async_remote_copy(
                src_ref=block(mid_q, t), dst_ref=block(mid_x, t), send_sem=x_send, recv_sem=x_recv.at[t // NB],
                device_id=dev(ahead, c), device_id_type=MESH,
            ).start()

    ld_cot.wait()
    ld_pw.wait()

    def part_chunk(f, _):
        weights = pw[pl.ds(pl.multiple_of(f * FW, FW), FW), :]

        def part_block(r, _):
            rows = pl.ds(pl.multiple_of(r * RB, RB), RB)
            part[f, rows, :] = dot_t(cot[rows, :], weights).astype(BF)
            t = f * NB + r

            @pl.when(t < WINDOW)
            def _():
                start_e(t)

            return 0

        return lax.fori_loop(0, NB, part_block, 0)

    part_chunk(0, 0)

    def clear_x():
        @pl.when(jnp.logical_not(has_src))
        def _():
            def clear(i, _):
                mid_x[i // 32, pl.ds(pl.multiple_of((i % 32) * 64, 64), 64), :] = jnp.zeros((64, FW), BF)
                return 0

            lax.fori_loop(0, 32 * NF, clear, 0)

    def service(t):
        wait_for(block(mid, t), e_recv.at[t])
        nxt = t + WINDOW

        @pl.when(nxt < NT)
        def _():
            start_e(nxt)

        f, r0 = t // NB, (t % NB) * RB

        def add(i, _):
            rows = pl.ds(pl.multiple_of(r0 + i * 64, 64), 64)
            mid[f, rows, :] = (part[f, rows, :].astype(F32) + mid[f, rows, :].astype(F32)).astype(BF)
            return 0

        lax.fori_loop(0, RB // 64, add, 0)
        start_q(t)

    def turn_rows():
        def turn(i, _):
            span = pl.ds(pl.multiple_of(i * 128, 128), 128)
            h_t[:, span] = io[span, :].T
            return 0

        lax.fori_loop(0, ROWS // 128, turn, 0)

    def proj_block(k):
        def proj_tile(i, _):
            rows = pl.ds(pl.multiple_of(i * 384, 384), 384)
            value = dot(h_t[rows, :], cot[:, k * 256:(k + 1) * 256])
            for j in range(384 // XS):
                spot = pl.ds(pl.multiple_of((i * (384 // XS) + j) * XP + k * XS, 8), XS)
                slab[0, 0, spot, :] = value[j * XS:(j + 1) * XS, :128]
                slab[0, 1, spot, :] = value[j * XS:(j + 1) * XS, 128:]
            return 0

        lax.fori_loop(0, 2, proj_tile, 0)

    def send(src, dst, send_sem, recv_sem, device):
        pltpu.make_async_remote_copy(
            src_ref=src, dst_ref=dst, send_sem=send_sem, recv_sem=recv_sem, device_id=device, device_id_type=MESH
        ).start()

    def core_send(g):
        def cast(i, _):
            rows = pl.ds(pl.multiple_of(i * 128, 128), 128)
            cs[g, rows, :] = slab[g % 2, 1 - core, rows, :].astype(BF)
            return 0

        lax.fori_loop(0, SLAB // 128, cast, 0)
        send(cs.at[g], cr.at[g], c_send, c_recv.at[g], twin)

    def a_exchange(g):
        wait_for(cr.at[g], c_recv.at[g])

        def add(i, _):
            rows = pl.ds(pl.multiple_of((1 - half) * ZH + i * 128, 128), 128)
            total = slab[g % 2, core, rows, :] + cr[g, rows, :].astype(F32)
            as_[g, pl.ds(pl.multiple_of(i * 128, 128), 128), :] = total.astype(BF)
            return 0

        lax.fori_loop(0, ZH // 128, add, 0)
        send(as_.at[g], ar.at[g], a_send, a_recv.at[g], dev_a)

    def quarter_sum(g, which, i):
        rows = pl.ds(pl.multiple_of(which * ZP + i * 64, 64), 64)
        inner = pl.ds(pl.multiple_of((which - 2 * half) * ZP + i * 64, 64), 64)
        return slab[g % 2, core, rows, :] + cr[g, rows, :].astype(F32) + ar[g, inner, :].astype(F32)

    def b_exchange(g):
        wait_for(ar.at[g], a_recv.at[g])

        def add(i, _):
            bs[g, pl.ds(pl.multiple_of(i * 64, 64), 64), :] = quarter_sum(g, other_quarter, i).astype(BF)
            return 0

        lax.fori_loop(0, ZP // 64, add, 0)
        send(bs.at[g], br.at[g], b_send, b_recv.at[g], dev_b)

    def x_exchange(g):
        wait_for(br.at[g], b_recv.at[g])

        def add(i, _):
            rows = pl.ds(pl.multiple_of(i * 64, 64), 64)
            z32[rows, :] = quarter_sum(g, quarter, i) + br[g, rows, :].astype(F32)
            return 0

        lax.fori_loop(0, ZP // 64, add, 0)
        for i in range(8):
            xs[g, i] = z32[i * XP:(i + 1) * XP, :].astype(BF)
        for d in range(1, 8):
            send(xs.at[g, p_peer(d)], xr.at[g, d - 1], xy_send, xy_recv.at[g], p_dev(d))

    def finish(g):
        wait_for(xr.at[g], xy_recv.at[g])
        total = z32[pl.ds(pl.multiple_of(p * XP, 8), XP), :]
        for d in range(7):
            total = total + xr[g, d].astype(F32)
        fin[g, core, quarter * 8 + p] = (total * SCALE).astype(BF)
        piece = fin.at[g, core, quarter * 8 + p]
        for d in range(1, 8):
            send(piece, piece, gx_send, gx_recv.at[g], p_dev(d))

    def gather_b(g):
        wait_for(xr.at[g], gx_recv.at[g])
        piece = fin.at[g, core, pl.ds(quarter * 8, 8)]
        send(piece, piece, gb_send, gb_recv.at[g], dev_b)

    def gather_a(g):
        wait_for(fin.at[g, core, pl.ds(0, 8)], gb_recv.at[g])
        piece = fin.at[g, core, pl.ds(half * 16, 16)]
        send(piece, piece, ga_send, ga_recv.at[g], dev_a)

    def gather_core(g):
        wait_for(fin.at[g, core, pl.ds(0, 16)], ga_recv.at[g])
        piece = fin.at[g, core]
        send(piece, piece, gc_send, gc_recv.at[g], twin)

    def write_out(g):
        wait_for(fin.at[g, 1 - core], gc_recv.at[g])
        for h in range(2):
            if g == 0:
                for k in range(3):
                    pltpu.make_async_copy(
                        fin.at[0, h, :, pl.ds(k * XS, XS), :],
                        gp_h.at[:, :, pl.ds(k * FW + h * 128, 128)], wout_sem,
                    ).start()
            else:
                pltpu.make_async_copy(
                    fin.at[g, h], gc_h.at[:, :, pl.ds((g - 1) * FW + h * 128, 128)], wout_sem
                ).start()

    def gelu(i):
        def tile(j, _):
            rows = pl.ds(pl.multiple_of(i * RB + j * 128, 128), 128)

            def strip(m, _):
                sub = pl.ds(pl.multiple_of(i * RB + j * 128 + m * 16, 16), 16)
                wide = io[sub, :].astype(F32)
                cumul = 0.5 * (1.0 + lax.erf(wide * (1.0 / math.sqrt(2.0))))
                dense = jnp.exp(-0.5 * wide * wide) * (1.0 / math.sqrt(2.0 * math.pi))
                der[sub, :] = cumul + wide * dense
                io[sub, :] = (wide * cumul).astype(BF)
                return 0

            lax.fori_loop(0, 8, strip, 0)
            h_t[:, rows] = io[rows, :].T
            return 0

        lax.fori_loop(0, RB // 128, tile, 0)

    for i in range(NB):
        service(i)
        if i >= LAG:
            forward_x(i - LAG)
        if i == 0:
            part_chunk(1, 0)
        elif i == 1:
            ld_cout.wait()
            turn_rows()
            ld_inp.start()
            clear_x()
        elif i == 2:
            proj_block(0)
            proj_block(1)
        elif i == 3:
            proj_block(2)
            core_send(0)
        elif i == 4:
            part_chunk(2, 0)
        elif i == 5:
            ld_inp.wait()
            gelu(0)
            a_exchange(0)
            gelu(1)
        elif i == 6:
            for r in (2, 3, 4):
                gelu(r)
        else:
            b_exchange(0)
            for r in (5, 6, 7):
                gelu(r)

    for cp in ld_cw:
        cp.wait()

    tap_q = 2 * yh
    tap_x = 2 - 2 * yh

    def weight_tap(f, tap, taps):
        def tile(i, _):
            rows = pl.ds(pl.multiple_of(i * 256, 256), 256)
            value = dot(h_t[rows, :], taps[f])
            spot = pl.ds(pl.multiple_of(tap * CH + i * 256, 256), 256)
            slab[(f + 1) % 2, 0, spot, :] = value[:, :128]
            slab[(f + 1) % 2, 1, spot, :] = value[:, 128:]
            return 0

        lax.fori_loop(0, CH // 256, tile, 0)

    def data_rows(g, first, count):
        f = g - 1

        def tile(i, _):
            rows = pl.ds(pl.multiple_of(i * RB, RB), RB)
            total = dot_t(mid[f, rows, :], cw[f, 1])
            total = total + dot_t(mid_q[f, rows, :], cw[f, tap_q])
            total = total + dot_t(mid_x[f, rows, :], cw[f, tap_x])

            @pl.when(g == 1)
            def _():
                gh[rows, :] = total

            @pl.when(g > 1)
            def _():
                gh[rows, :] = gh[rows, :] + total

            @pl.when(g == NF)
            def _():
                def strip(m, _):
                    sub = pl.ds(pl.multiple_of(i * RB + m * 16, 16), 16)
                    io[sub, :] = (cot[sub, :].astype(F32) + gh[sub, :] * der[sub, :]).astype(BF)
                    return 0

                lax.fori_loop(0, RB // 16, strip, 0)
                pltpu.make_async_copy(io.at[rows], gi_h.at[rows], out_sem).start()

            return 0

        lax.fori_loop(first, first + count, tile, 0)

    def phase(g, _):
        f = g - 1

        def serve(i):
            t = g * NB + i

            @pl.when(g < NF)
            def _():
                service(t)

            if i < LAG:
                forward_x(t - LAG)
            else:
                @pl.when(g < NF)
                def _():
                    forward_x(t - LAG)

        serve(0)
        weight_tap(f, 1, mid)
        serve(1)
        x_exchange(g - 1)
        weight_tap(f, tap_q, mid_q)
        serve(2)
        finish(g - 1)

        @pl.when(g == 2)
        def _():
            write_out(0)

        @pl.when(g == 3)
        def _():
            write_out(1)

        serve(3)

        @pl.when(has_src)
        def _():
            wait_for(mid_x.at[f], x_recv.at[f])

        weight_tap(f, tap_x, mid_x)
        core_send(g)
        serve(4)
        gather_b(g - 1)
        data_rows(g, 0, 2)
        serve(5)
        a_exchange(g)
        data_rows(g, 2, 2)
        serve(6)
        gather_a(g - 1)
        data_rows(g, 4, 2)
        serve(7)
        b_exchange(g)
        gather_core(g - 1)
        data_rows(g, 6, 2)
        return 0

    lax.fori_loop(1, NF + 1, phase, 0)
    x_exchange(NF)
    finish(NF)
    write_out(NF - 1)
    gather_b(NF)
    gather_a(NF)
    gather_core(NF)
    write_out(NF)

    wait_for(part, e_send)
    wait_for(mid, q_send)

    @pl.when(has_dst)
    def _():
        wait_for(mid_q, x_send)

    wait_for(cs, c_send)
    wait_for(as_, a_send)
    wait_for(bs, b_send)
    wait_for(xr, xy_send)
    wait_for(xr, gx_send)
    for g in range(NF + 1):
        wait_for(fin.at[g, 0, pl.ds(0, 8)], gb_send)
        wait_for(fin.at[g, 0, pl.ds(0, 16)], ga_send)
        wait_for(fin.at[g, 0], gc_send)
    wait_for(io, out_sem)
    wait_for(fin, wout_sem)


def shards(inputs, cotangent, conv_out, conv_weight, proj_weight):
    any_spec = pl.BlockSpec(memory_space=pl.ANY)
    dma = pltpu.SemaphoreType.DMA
    slabs = NF + 1
    rows_bf = pltpu.VMEM((ROWS, CH), BF)
    chunks = pltpu.VMEM((NF, ROWS, FW), BF)
    flat = [a.reshape(ROWS, CH) for a in (inputs, cotangent, conv_out)]
    grad_inputs, grad_conv, grad_proj = pl.pallas_call(
        kernel,
        out_shape=(
            jax.ShapeDtypeStruct((ROWS, CH), BF),
            jax.ShapeDtypeStruct((32, XP, FULL), BF),
            jax.ShapeDtypeStruct((32, XS, CH), BF),
        ),
        in_specs=[any_spec] * 5,
        out_specs=(any_spec,) * 3,
        scratch_shapes=[
            rows_bf, rows_bf, pltpu.VMEM((CH, ROWS), BF), pltpu.VMEM((ROWS, CH), F32),
            pltpu.VMEM((FULL, CH), BF), pltpu.VMEM((NF, 3, CH, FW), BF),
            chunks, chunks, chunks, chunks, pltpu.VMEM((ROWS, CH), F32),
            pltpu.VMEM((2, 2, SLAB, 128), F32), pltpu.VMEM((ZP, 128), F32),
            pltpu.VMEM((slabs, SLAB, 128), BF), pltpu.VMEM((slabs, SLAB, 128), BF),
            pltpu.VMEM((slabs, ZH, 128), BF), pltpu.VMEM((slabs, ZH, 128), BF),
            pltpu.VMEM((slabs, ZP, 128), BF), pltpu.VMEM((slabs, ZP, 128), BF),
            pltpu.VMEM((slabs, 8, XP, 128), BF), pltpu.VMEM((slabs, 7, XP, 128), BF),
            pltpu.VMEM((slabs, 2, 32, XP, 128), BF),
            dma((4 + NF,)), dma, dma,
            dma, dma((NT,)), dma, dma((NT,)), dma, dma((NF,)),
        ] + [dma, dma((slabs,))] * 8,
        compiler_params=pltpu.CompilerParams(
            collective_id=0, has_side_effects=True, vmem_limit_bytes=62 * 1024 * 1024
        ),
    )(*flat, conv_weight, proj_weight)
    grad_conv = grad_conv.reshape(3, CH, FULL)
    grad_proj = grad_proj.reshape(FULL, CH)
    return (grad_inputs.reshape(inputs.shape), grad_conv, grad_proj)


def solution(mesh):
    in_specs = (
        P(None, "seq", "ch"),
        P(None, "seq", "ch"),
        P(None, "seq", None),
        P(None, "ch", None),
        P(None, "ch"),
    )
    out_specs = (P(None, "seq", "ch"), P(None, "ch", None), P(None, "ch"))
    return jax.shard_map(shards, mesh=mesh, in_specs=in_specs, out_specs=out_specs, check_vma=False)
```

```python
import functools
import math

import jax
import jax.numpy as jnp
from jax import lax
from jax.experimental import pallas as pl
from jax.experimental.pallas import tpu as pltpu
from jax.sharding import PartitionSpec as P

MESH = pl.DeviceIdType.MESH
ROWS = 2048
CH = 768
FULL = 768
FW = 256
NF = FULL // FW
RB = 256
NB = ROWS // RB
NT = NF * NB
WINDOW = 6
LAG = 2
X_TICK = 5
TICKS = (
    (3, 5, 22, 24, 25, 26, 27, 28, 29, 30),
    (13, 15, 22, 24, 25, 26, 27, 28, 29, 30),
    (21, 23, 24, 25, 26, 27, 28, 29, 30, 31),
    (27, 28, 28, 29, 30, 31, 32, 33, 34, 35),
)
AXES = (0, 1, 0, 1)
SLAB = 3 * CH
ZH = SLAB // 2
ZP = SLAB // 4
XP = ZP // 8
XS = XP // 3
SCALE = 1.0 / math.sqrt(131072.0)
BF = jnp.bfloat16
F32 = jnp.float32


def dot(a, b):
    return lax.dot_general(a, b, (((1,), (0,)), ((), ())), preferred_element_type=F32)


def dot_t(a, b):
    return lax.dot_general(a, b, (((1,), (1,)), ((), ())), preferred_element_type=F32)


def wait_for(ref, sem):
    pltpu.make_async_copy(ref, ref, sem).wait()


def kernel(
    inp_h, cot_h, cout_h, cw_h, pw_h, gi_h, gc_h, gp_h,
    cot, io, h_t, der, pw, cw, part, mid, mid_q, mid_x, gh,
    slab, keep, z32, cs, cr, as_, ar, bs, br, xs, xr, fin,
    ld_sem, out_sem, wout_sem,
    e_send, e_recv, q_send, q_recv, x_send, x_recv,
    c_send, c_recv, a_send, a_recv, b_send, b_recv, xy_send, xy_recv,
    gx_send, gx_recv, gb_send, gb_recv, ga_send, ga_recv, gc_send, gc_recv,
):
    s = lax.axis_index("seq")
    c = lax.axis_index("ch")
    core = s % 2
    yh = (s // 2) % 2
    z = s // 16

    def dev(seq, ch):
        return {"seq": seq, "ch": ch}

    partner = dev(s, 1 - c)
    across = dev(s + 2 - 4 * yh, 1 - c)
    ahead = s + 4 - 8 * yh
    behind = s - 4 + 8 * yh
    has_dst = jnp.logical_and(ahead >= 0, ahead < 64)
    has_src = jnp.logical_and(behind >= 0, behind < 64)
    twin = dev(s + 1 - 2 * core, c)

    x = (s // 4) % 4

    def geometry(i, j, axis):
        def at_axis(k):
            return dev(k * 16 + s % 16 if axis == 0 else z * 16 + k * 4 + s % 4, c)

        following, mirror = i + 1 - 2 * (i % 2), 3 - i
        upper, middle = i // 2, ((i + 1) // 2) % 2
        half = middle + core * (upper - middle)
        quarter = 2 * half + upper + core * (i % 2 - upper)
        place = j * 2 + yh

        def peer(d):
            return (place + d) % 8

        def peer_dev(d):
            jj, yy = peer(d) // 2, peer(d) % 2
            return dev(z * 16 + jj * 4 + yy * 2 + core if axis == 0 else jj * 16 + x * 4 + yy * 2 + core, c)

        return dict(
            dev_a=at_axis(following + core * (mirror - following)), dev_b=at_axis(mirror + core * (following - mirror)),
            half=half, quarter=quarter, other=4 * half + 1 - quarter, place=place, peer=peer, peer_dev=peer_dev,
        )

    geometries = (geometry(z, x, 0), geometry(x, z, 1))

    ld_cot = pltpu.make_async_copy(cot_h, cot, ld_sem.at[0])
    ld_pw = pltpu.make_async_copy(pw_h, pw, ld_sem.at[1])
    ld_cout = pltpu.make_async_copy(cout_h, io, ld_sem.at[2])
    ld_inp = pltpu.make_async_copy(inp_h, io, ld_sem.at[3])
    ld_cw = [
        pltpu.make_async_copy(cw_h.at[:, :, pl.ds(f * FW, FW)], cw.at[f], ld_sem.at[4 + f])
        for f in range(NF)
    ]
    ld_cot.start()
    ld_pw.start()
    ld_cout.start()
    for cp in ld_cw:
        cp.start()

    barrier = pltpu.get_barrier_semaphore()

    def greet(device):
        pl.semaphore_signal(barrier, inc=1, device_id=device, device_id_type=MESH)

    greet(partner)
    greet(across)
    greet(twin)
    for d in range(1, 8):
        greet(geometries[0]["peer_dev"](d))
    for d in range(1, 4):
        for other_yh in range(2):
            greet(dev(((z + d) % 4) * 16 + x * 4 + other_yh * 2 + core, c))

    far_dst = jnp.logical_and(has_dst, ahead // 16 != z)
    far_src = jnp.logical_and(has_src, behind // 16 != z)

    @pl.when(far_dst)
    def _():
        greet(dev(ahead, c))

    @pl.when(far_src)
    def _():
        greet(dev(behind, c))

    pl.semaphore_wait(barrier, 16 + far_dst.astype(jnp.int32) + far_src.astype(jnp.int32))

    def block(ref, t):
        return ref.at[t // NB, pl.ds(pl.multiple_of((t % NB) * RB, RB), RB)]

    def start_e(t):
        pltpu.make_async_remote_copy(
            src_ref=block(part, t), dst_ref=block(mid, t), send_sem=e_send, recv_sem=e_recv.at[t],
            device_id=partner, device_id_type=MESH,
        ).start()

    def start_q(t):
        pltpu.make_async_remote_copy(
            src_ref=block(mid, t), dst_ref=block(mid_q, t), send_sem=q_send, recv_sem=q_recv.at[t],
            device_id=across, device_id_type=MESH,
        ).start()

    def forward_x(t):
        wait_for(block(mid_q, t), q_recv.at[t])

        @pl.when(has_dst)
        def _():
            pltpu.make_async_remote_copy(
                src_ref=block(mid_q, t), dst_ref=block(mid_x, t), send_sem=x_send, recv_sem=x_recv.at[t // NB],
                device_id=dev(ahead, c), device_id_type=MESH,
            ).start()

    ld_cot.wait()
    ld_pw.wait()

    def part_chunk(f, _):
        weights = pw[pl.ds(pl.multiple_of(f * FW, FW), FW), :]

        def part_block(r, _):
            rows = pl.ds(pl.multiple_of(r * RB, RB), RB)
            part[f, rows, :] = dot_t(cot[rows, :], weights).astype(BF)
            t = f * NB + r

            @pl.when(t < WINDOW)
            def _():
                start_e(t)

            return 0

        return lax.fori_loop(0, NB, part_block, 0)

    part_chunk(0, 0)

    def clear_x():
        @pl.when(jnp.logical_not(has_src))
        def _():
            def clear(i, _):
                mid_x[i // 32, pl.ds(pl.multiple_of((i % 32) * 64, 64), 64), :] = jnp.zeros((64, FW), BF)
                return 0

            lax.fori_loop(0, 32 * NF, clear, 0)

    def service(t):
        wait_for(block(mid, t), e_recv.at[t])
        nxt = t + WINDOW

        @pl.when(nxt < NT)
        def _():
            start_e(nxt)

        f, r0 = t // NB, (t % NB) * RB

        def add(i, _):
            rows = pl.ds(pl.multiple_of(r0 + i * 64, 64), 64)
            mid[f, rows, :] = (part[f, rows, :].astype(F32) + mid[f, rows, :].astype(F32)).astype(BF)
            return 0

        lax.fori_loop(0, RB // 64, add, 0)
        start_q(t)

    def turn_rows():
        def turn(i, _):
            span = pl.ds(pl.multiple_of(i * 128, 128), 128)
            h_t[:, span] = io[span, :].T
            return 0

        lax.fori_loop(0, ROWS // 128, turn, 0)

    def proj_block(k):
        def proj_tile(i, _):
            rows = pl.ds(pl.multiple_of(i * 384, 384), 384)
            value = dot(h_t[rows, :], cot[:, k * 256:(k + 1) * 256])
            for j in range(384 // XS):
                spot = pl.ds(pl.multiple_of((i * (384 // XS) + j) * XP + k * XS, 8), XS)
                slab[0, spot, :] = value[j * XS:(j + 1) * XS, :128]
                slab[1, spot, :] = value[j * XS:(j + 1) * XS, 128:]
            return 0

        lax.fori_loop(0, 2, proj_tile, 0)

    def send(src, dst, send_sem, recv_sem, device):
        pltpu.make_async_remote_copy(
            src_ref=src, dst_ref=dst, send_sem=send_sem, recv_sem=recv_sem, device_id=device, device_id_type=MESH
        ).start()

    def core_send(g):
        def cast(i, _):
            rows = pl.ds(pl.multiple_of(i * 128, 128), 128)
            cs[g, rows, :] = slab[1 - core, rows, :].astype(BF)
            return 0

        lax.fori_loop(0, SLAB // 128, cast, 0)
        send(cs.at[g], cr.at[g], c_send, c_recv.at[g], twin)

    def core_sum(g):
        half = geometries[AXES[g]]["half"]
        wait_for(cr.at[g], c_recv.at[g])

        def add(i, _):
            inner = pl.ds(pl.multiple_of(i * 128, 128), 128)
            mine = pl.ds(pl.multiple_of(half * ZH + i * 128, 128), 128)
            other = pl.ds(pl.multiple_of((1 - half) * ZH + i * 128, 128), 128)
            keep[g, inner, :] = slab[core, mine, :] + cr[g, mine, :].astype(F32)
            as_[g, inner, :] = (slab[core, other, :] + cr[g, other, :].astype(F32)).astype(BF)
            return 0

        lax.fori_loop(0, ZH // 128, add, 0)

    def a_exchange(g):
        send(as_.at[g], ar.at[g], a_send, a_recv.at[g], geometries[AXES[g]]["dev_a"])

    def quarter_sum(g, which, i):
        half = geometries[AXES[g]]["half"]
        inner = pl.ds(pl.multiple_of((which - 2 * half) * ZP + i * 64, 64), 64)
        return keep[g, inner, :] + ar[g, inner, :].astype(F32)

    def b_exchange(g):
        wait_for(ar.at[g], a_recv.at[g])

        def add(i, _):
            total = quarter_sum(g, geometries[AXES[g]]["other"], i)
            bs[g, pl.ds(pl.multiple_of(i * 64, 64), 64), :] = total.astype(BF)
            return 0

        lax.fori_loop(0, ZP // 64, add, 0)
        send(bs.at[g], br.at[g], b_send, b_recv.at[g], geometries[AXES[g]]["dev_b"])

    def x_exchange(g):
        geo = geometries[AXES[g]]
        wait_for(br.at[g], b_recv.at[g])

        def add(i, _):
            rows = pl.ds(pl.multiple_of(i * 64, 64), 64)
            z32[g, rows, :] = quarter_sum(g, geo["quarter"], i) + br[g, rows, :].astype(F32)
            return 0

        lax.fori_loop(0, ZP // 64, add, 0)
        for i in range(8):
            xs[g, i] = z32[g, i * XP:(i + 1) * XP, :].astype(BF)
        for d in range(1, 8):
            send(xs.at[g, geo["peer"](d)], xr.at[g, d - 1], xy_send, xy_recv.at[g], geo["peer_dev"](d))

    def finish(g):
        geo = geometries[AXES[g]]
        wait_for(xr.at[g], xy_recv.at[g])
        total = z32[g, pl.ds(pl.multiple_of(geo["place"] * XP, 8), XP), :]
        for d in range(7):
            total = total + xr[g, d].astype(F32)
        fin[g, core, geo["quarter"] * 8 + geo["place"]] = (total * SCALE).astype(BF)
        piece = fin.at[g, core, geo["quarter"] * 8 + geo["place"]]
        for d in range(1, 8):
            send(piece, piece, gx_send, gx_recv.at[g], geo["peer_dev"](d))

    def gather_b(g):
        geo = geometries[AXES[g]]
        wait_for(xr.at[g], gx_recv.at[g])
        piece = fin.at[g, core, pl.ds(geo["quarter"] * 8, 8)]
        send(piece, piece, gb_send, gb_recv.at[g], geo["dev_b"])

    def gather_a(g):
        geo = geometries[AXES[g]]
        wait_for(fin.at[g, core, pl.ds(0, 8)], gb_recv.at[g])
        piece = fin.at[g, core, pl.ds(geo["half"] * 16, 16)]
        send(piece, piece, ga_send, ga_recv.at[g], geo["dev_a"])

    def gather_core(g):
        wait_for(fin.at[g, core, pl.ds(0, 16)], ga_recv.at[g])
        piece = fin.at[g, core]
        send(piece, piece, gc_send, gc_recv.at[g], twin)

    def write_out(g):
        wait_for(fin.at[g, 1 - core], gc_recv.at[g])
        for h in range(2):
            if g == 0:
                for k in range(3):
                    pltpu.make_async_copy(
                        fin.at[0, h, :, pl.ds(k * XS, XS), :],
                        gp_h.at[:, :, pl.ds(k * FW + h * 128, 128)], wout_sem,
                    ).start()
            else:
                pltpu.make_async_copy(
                    fin.at[g, h], gc_h.at[:, :, pl.ds((g - 1) * FW + h * 128, 128)], wout_sem
                ).start()

    def gelu(i):
        def tile(j, _):
            rows = pl.ds(pl.multiple_of(i * RB + j * 128, 128), 128)

            def strip(m, _):
                sub = pl.ds(pl.multiple_of(i * RB + j * 128 + m * 16, 16), 16)
                wide = io[sub, :].astype(F32)
                cumul = 0.5 * (1.0 + lax.erf(wide * (1.0 / math.sqrt(2.0))))
                dense = jnp.exp(-0.5 * wide * wide) * (1.0 / math.sqrt(2.0 * math.pi))
                der[sub, :] = cumul + wide * dense
                io[sub, :] = (wide * cumul).astype(BF)
                return 0

            lax.fori_loop(0, 8, strip, 0)
            h_t[:, rows] = io[rows, :].T
            return 0

        lax.fori_loop(0, RB // 128, tile, 0)

    tap_q = 2 * yh
    tap_x = 2 - 2 * yh

    def weight_tap(f, tap, taps):
        def tile(i, _):
            rows = pl.ds(pl.multiple_of(i * 256, 256), 256)
            value = dot(h_t[rows, :], taps[f])
            spot = pl.ds(pl.multiple_of(tap * CH + i * 256, 256), 256)
            slab[0, spot, :] = value[:, :128]
            slab[1, spot, :] = value[:, 128:]
            return 0

        lax.fori_loop(0, CH // 256, tile, 0)

    def data_rows(f, first, count):
        def tile(i, _):
            rows = pl.ds(pl.multiple_of(i * RB, RB), RB)
            total = dot_t(mid[f, rows, :], cw[f, 1])
            total = total + dot_t(mid_q[f, rows, :], cw[f, tap_q])
            total = total + dot_t(mid_x[f, rows, :], cw[f, tap_x])
            gh[rows, :] = total if f == 0 else gh[rows, :] + total
            if f == NF - 1:
                def strip(m, _):
                    sub = pl.ds(pl.multiple_of(i * RB + m * 16, 16), 16)
                    io[sub, :] = (cot[sub, :].astype(F32) + gh[sub, :] * der[sub, :]).astype(BF)
                    return 0

                lax.fori_loop(0, RB // 16, strip, 0)
                pltpu.make_async_copy(io.at[rows], gi_h.at[rows], out_sem).start()
            return 0

        lax.fori_loop(first, first + count, tile, 0)

    def x_tap(f):
        @pl.when(has_src)
        def _():
            wait_for(mid_x.at[f], x_recv.at[f])

        weight_tap(f, tap_x, mid_x)

    def prepare():
        ld_cout.wait()
        turn_rows()
        ld_inp.start()
        clear_x()

    def load_done():
        ld_inp.wait()
        for cp in ld_cw:
            cp.wait()

    stages = (
        core_send, core_sum, a_exchange, b_exchange, x_exchange, finish, gather_b, gather_a, gather_core, write_out
    )
    plan = {}

    def at(tick, action, *args):
        plan.setdefault(tick, []).append((action, args))

    at(0, part_chunk, 1, 0)
    at(1, prepare)
    at(2, proj_block, 0)
    at(2, proj_block, 1)
    at(3, proj_block, 2)
    at(4, part_chunk, 2, 0)
    at(5, load_done)
    for i in range(NB):
        at((5, 5, 6, 6, 6, 7, 7, 7)[i], gelu, i)
    for f in range(NF):
        base = NB * (f + 1)
        at(base, weight_tap, f, 1, mid)
        at(base + 1, weight_tap, f, tap_q, mid_q)
        at(base + X_TICK if f < NF - 1 else base + 3, x_tap, f)
    for g in range(NF + 1):
        for n, tick in enumerate(TICKS[g]):
            at(tick, stages[n], g)
    for f in range(NF):
        for i in range(4):
            at((NB * (f + 1) + X_TICK if f < NF - 1 else 27) + i, data_rows, f, 2 * i, 2)
    for tick in range(max(NT + LAG - 1, max(plan)) + 1):
        if tick < NT:
            service(tick)
        if LAG <= tick < NT + LAG:
            forward_x(tick - LAG)
        for action, args in plan.get(tick, ()):
            action(*args)

    wait_for(part, e_send)
    wait_for(mid, q_send)

    @pl.when(has_dst)
    def _():
        wait_for(mid_q, x_send)

    wait_for(cs, c_send)
    wait_for(as_, a_send)
    wait_for(bs, b_send)
    wait_for(xr, xy_send)
    wait_for(xr, gx_send)
    for g in range(NF + 1):
        wait_for(fin.at[g, 0, pl.ds(0, 8)], gb_send)
        wait_for(fin.at[g, 0, pl.ds(0, 16)], ga_send)
        wait_for(fin.at[g, 0], gc_send)
    wait_for(io, out_sem)
    wait_for(fin, wout_sem)


def shards(inputs, cotangent, conv_out, conv_weight, proj_weight):
    any_spec = pl.BlockSpec(memory_space=pl.ANY)
    dma = pltpu.SemaphoreType.DMA
    slabs = NF + 1
    rows_bf = pltpu.VMEM((ROWS, CH), BF)
    chunks = pltpu.VMEM((NF, ROWS, FW), BF)
    flat = [a.reshape(ROWS, CH) for a in (inputs, cotangent, conv_out)]
    grad_inputs, grad_conv, grad_proj = pl.pallas_call(
        kernel,
        out_shape=(
            jax.ShapeDtypeStruct((ROWS, CH), BF),
            jax.ShapeDtypeStruct((32, XP, FULL), BF),
            jax.ShapeDtypeStruct((32, XS, CH), BF),
        ),
        in_specs=[any_spec] * 5,
        out_specs=(any_spec,) * 3,
        scratch_shapes=[
            rows_bf, rows_bf, pltpu.VMEM((CH, ROWS), BF), pltpu.VMEM((ROWS, CH), F32),
            pltpu.VMEM((FULL, CH), BF), pltpu.VMEM((NF, 3, CH, FW), BF),
            chunks, chunks, chunks, chunks, pltpu.VMEM((ROWS, CH), F32),
            pltpu.VMEM((2, SLAB, 128), F32), pltpu.VMEM((slabs, ZH, 128), F32), pltpu.VMEM((slabs, ZP, 128), F32),
            pltpu.VMEM((slabs, SLAB, 128), BF), pltpu.VMEM((slabs, SLAB, 128), BF),
            pltpu.VMEM((slabs, ZH, 128), BF), pltpu.VMEM((slabs, ZH, 128), BF),
            pltpu.VMEM((slabs, ZP, 128), BF), pltpu.VMEM((slabs, ZP, 128), BF),
            pltpu.VMEM((slabs, 8, XP, 128), BF), pltpu.VMEM((slabs, 7, XP, 128), BF),
            pltpu.VMEM((slabs, 2, 32, XP, 128), BF),
            dma((4 + NF,)), dma, dma,
            dma, dma((NT,)), dma, dma((NT,)), dma, dma((NF,)),
        ] + [dma, dma((slabs,))] * 8,
        compiler_params=pltpu.CompilerParams(
            collective_id=0, has_side_effects=True, vmem_limit_bytes=62 * 1024 * 1024
        ),
    )(*flat, conv_weight, proj_weight)
    grad_conv = grad_conv.reshape(3, CH, FULL)
    grad_proj = grad_proj.reshape(FULL, CH)
    return (grad_inputs.reshape(inputs.shape), grad_conv, grad_proj)


def solution(mesh):
    in_specs = (
        P(None, "seq", "ch"),
        P(None, "seq", "ch"),
        P(None, "seq", None),
        P(None, "ch", None),
        P(None, "ch"),
    )
    out_specs = (P(None, "seq", "ch"), P(None, "ch", None), P(None, "ch"))
    return jax.shard_map(shards, mesh=mesh, in_specs=in_specs, out_specs=out_specs, check_vma=False)
```

```python
import functools
import math

import jax
import jax.numpy as jnp
from jax import lax
from jax.experimental import pallas as pl
from jax.experimental.pallas import tpu as pltpu
from jax.sharding import PartitionSpec as P

MESH = pl.DeviceIdType.MESH
ROWS = 2048
CH = 768
FULL = 768
FW = 256
NF = FULL // FW
RB = 256
NB = ROWS // RB
NT = NF * NB
WINDOW = 6
LAG = 2
X_TICK = 5
TICKS = (
    (3, 5, 28, 29, 30, 31, 32, 33, 34, 35),
    (13, 15, 28, 29, 30, 31, 32, 33, 34, 35),
    (21, 23, 26, 28, 29, 30, 31, 32, 33, 34),
    (27, 28, 28, 29, 30, 31, 32, 33, 34, 35),
)
AXES = (0, 1, 0, 1)
SLAB = 3 * CH
ZH = SLAB // 2
ZP = SLAB // 4
XP = ZP // 8
XS = XP // 3
SCALE = 1.0 / math.sqrt(131072.0)
BF = jnp.bfloat16
F32 = jnp.float32


def dot(a, b):
    return lax.dot_general(a, b, (((1,), (0,)), ((), ())), preferred_element_type=F32)


def dot_t(a, b):
    return lax.dot_general(a, b, (((1,), (1,)), ((), ())), preferred_element_type=F32)


def wait_for(ref, sem):
    pltpu.make_async_copy(ref, ref, sem).wait()


def kernel(
    inp_h, cot_h, cout_h, cw_h, pw_h, gi_h, gc_h, gp_h,
    cot, io, h_t, der, pw, cw, part, mid, mid_q, mid_x, gh,
    slab, keep, z32, cs, cr, as_, ar, bs, br, xs, xr, fin,
    ld_sem, out_sem, wout_sem,
    e_send, e_recv, q_send, q_recv, x_send, x_recv,
    c_send, c_recv, a_send, a_recv, b_send, b_recv, xy_send, xy_recv,
    gx_send, gx_recv, gb_send, gb_recv, ga_send, ga_recv, gc_send, gc_recv,
):
    s = lax.axis_index("seq")
    c = lax.axis_index("ch")
    core = s % 2
    yh = (s // 2) % 2
    z = s // 16

    def dev(seq, ch):
        return {"seq": seq, "ch": ch}

    partner = dev(s, 1 - c)
    across = dev(s + 2 - 4 * yh, 1 - c)
    ahead = s + 4 - 8 * yh
    behind = s - 4 + 8 * yh
    has_dst = jnp.logical_and(ahead >= 0, ahead < 64)
    has_src = jnp.logical_and(behind >= 0, behind < 64)
    twin = dev(s + 1 - 2 * core, c)

    x = (s // 4) % 4

    def geometry(i, j, axis):
        def at_axis(k):
            return dev(k * 16 + s % 16 if axis == 0 else z * 16 + k * 4 + s % 4, c)

        following, mirror = i + 1 - 2 * (i % 2), 3 - i
        upper, middle = i // 2, ((i + 1) // 2) % 2
        half = middle + core * (upper - middle)
        quarter = 2 * half + upper + core * (i % 2 - upper)
        place = j * 2 + yh

        def peer(d):
            return (place + d) % 8

        def peer_dev(d):
            jj, yy = peer(d) // 2, peer(d) % 2
            return dev(z * 16 + jj * 4 + yy * 2 + core if axis == 0 else jj * 16 + x * 4 + yy * 2 + core, c)

        return dict(
            dev_a=at_axis(following + core * (mirror - following)), dev_b=at_axis(mirror + core * (following - mirror)),
            half=half, quarter=quarter, other=4 * half + 1 - quarter, place=place, peer=peer, peer_dev=peer_dev,
        )

    geometries = (geometry(z, x, 0), geometry(x, z, 1))

    ld_cot = pltpu.make_async_copy(cot_h, cot, ld_sem.at[0])
    ld_pw = pltpu.make_async_copy(pw_h, pw, ld_sem.at[1])
    ld_cout = pltpu.make_async_copy(cout_h, io, ld_sem.at[2])
    ld_inp = pltpu.make_async_copy(inp_h, io, ld_sem.at[3])
    ld_cw = [
        pltpu.make_async_copy(cw_h.at[:, :, pl.ds(f * FW, FW)], cw.at[f], ld_sem.at[4 + f])
        for f in range(NF)
    ]
    ld_cot.start()
    ld_pw.start()
    ld_cout.start()
    for cp in ld_cw:
        cp.start()

    barrier = pltpu.get_barrier_semaphore()

    def greet(device):
        pl.semaphore_signal(barrier, inc=1, device_id=device, device_id_type=MESH)

    greet(partner)
    greet(across)
    greet(twin)
    for d in range(1, 8):
        greet(geometries[0]["peer_dev"](d))
    for d in range(1, 4):
        for other_yh in range(2):
            greet(dev(((z + d) % 4) * 16 + x * 4 + other_yh * 2 + core, c))

    far_dst = jnp.logical_and(has_dst, ahead // 16 != z)
    far_src = jnp.logical_and(has_src, behind // 16 != z)

    @pl.when(far_dst)
    def _():
        greet(dev(ahead, c))

    @pl.when(far_src)
    def _():
        greet(dev(behind, c))

    pl.semaphore_wait(barrier, 16 + far_dst.astype(jnp.int32) + far_src.astype(jnp.int32))

    def block(ref, t):
        return ref.at[t // NB, pl.ds(pl.multiple_of((t % NB) * RB, RB), RB)]

    def start_e(t):
        pltpu.make_async_remote_copy(
            src_ref=block(part, t), dst_ref=block(mid, t), send_sem=e_send, recv_sem=e_recv.at[t],
            device_id=partner, device_id_type=MESH,
        ).start()

    def start_q(t):
        pltpu.make_async_remote_copy(
            src_ref=block(mid, t), dst_ref=block(mid_q, t), send_sem=q_send, recv_sem=q_recv.at[t],
            device_id=across, device_id_type=MESH,
        ).start()

    def forward_x(t):
        wait_for(block(mid_q, t), q_recv.at[t])

        @pl.when(has_dst)
        def _():
            pltpu.make_async_remote_copy(
                src_ref=block(mid_q, t), dst_ref=block(mid_x, t), send_sem=x_send, recv_sem=x_recv.at[t // NB],
                device_id=dev(ahead, c), device_id_type=MESH,
            ).start()

    ld_cot.wait()
    ld_pw.wait()

    def part_chunk(f, _):
        weights = pw[pl.ds(pl.multiple_of(f * FW, FW), FW), :]

        def part_block(r, _):
            rows = pl.ds(pl.multiple_of(r * RB, RB), RB)
            part[f, rows, :] = dot_t(cot[rows, :], weights).astype(BF)
            t = f * NB + r

            @pl.when(t < WINDOW)
            def _():
                start_e(t)

            return 0

        return lax.fori_loop(0, NB, part_block, 0)

    part_chunk(0, 0)

    def clear_x():
        @pl.when(jnp.logical_not(has_src))
        def _():
            def clear(i, _):
                mid_x[i // 32, pl.ds(pl.multiple_of((i % 32) * 64, 64), 64), :] = jnp.zeros((64, FW), BF)
                return 0

            lax.fori_loop(0, 32 * NF, clear, 0)

    def service(t):
        wait_for(block(mid, t), e_recv.at[t])
        nxt = t + WINDOW

        @pl.when(nxt < NT)
        def _():
            start_e(nxt)

        f, r0 = t // NB, (t % NB) * RB

        def add(i, _):
            rows = pl.ds(pl.multiple_of(r0 + i * 64, 64), 64)
            mid[f, rows, :] = (part[f, rows, :].astype(F32) + mid[f, rows, :].astype(F32)).astype(BF)
            return 0

        lax.fori_loop(0, RB // 64, add, 0)
        start_q(t)

    def turn_rows():
        def turn(i, _):
            span = pl.ds(pl.multiple_of(i * 128, 128), 128)
            h_t[:, span] = io[span, :].T
            return 0

        lax.fori_loop(0, ROWS // 128, turn, 0)

    def proj_block(k):
        def proj_tile(i, _):
            rows = pl.ds(pl.multiple_of(i * 384, 384), 384)
            value = dot(h_t[rows, :], cot[:, k * 256:(k + 1) * 256])
            for j in range(384 // XS):
                spot = pl.ds(pl.multiple_of((i * (384 // XS) + j) * XP + k * XS, 8), XS)
                slab[0, spot, :] = value[j * XS:(j + 1) * XS, :128]
                slab[1, spot, :] = value[j * XS:(j + 1) * XS, 128:]
            return 0

        lax.fori_loop(0, 2, proj_tile, 0)

    def send(src, dst, send_sem, recv_sem, device):
        pltpu.make_async_remote_copy(
            src_ref=src, dst_ref=dst, send_sem=send_sem, recv_sem=recv_sem, device_id=device, device_id_type=MESH
        ).start()

    def core_send(g):
        def cast(i, _):
            rows = pl.ds(pl.multiple_of(i * 128, 128), 128)
            cs[g, rows, :] = slab[1 - core, rows, :].astype(BF)
            return 0

        lax.fori_loop(0, SLAB // 128, cast, 0)
        send(cs.at[g], cr.at[g], c_send, c_recv.at[g], twin)

    def core_sum(g):
        half = geometries[AXES[g]]["half"]
        wait_for(cr.at[g], c_recv.at[g])

        def add(i, _):
            inner = pl.ds(pl.multiple_of(i * 128, 128), 128)
            mine = pl.ds(pl.multiple_of(half * ZH + i * 128, 128), 128)
            other = pl.ds(pl.multiple_of((1 - half) * ZH + i * 128, 128), 128)
            keep[g, inner, :] = slab[core, mine, :] + cr[g, mine, :].astype(F32)
            as_[g, inner, :] = (slab[core, other, :] + cr[g, other, :].astype(F32)).astype(BF)
            return 0

        lax.fori_loop(0, ZH // 128, add, 0)

    def a_exchange(g):
        send(as_.at[g], ar.at[g], a_send, a_recv.at[g], geometries[AXES[g]]["dev_a"])

    def quarter_sum(g, which, i):
        half = geometries[AXES[g]]["half"]
        inner = pl.ds(pl.multiple_of((which - 2 * half) * ZP + i * 64, 64), 64)
        return keep[g, inner, :] + ar[g, inner, :].astype(F32)

    def b_exchange(g):
        wait_for(ar.at[g], a_recv.at[g])

        def add(i, _):
            total = quarter_sum(g, geometries[AXES[g]]["other"], i)
            bs[g, pl.ds(pl.multiple_of(i * 64, 64), 64), :] = total.astype(BF)
            return 0

        lax.fori_loop(0, ZP // 64, add, 0)
        send(bs.at[g], br.at[g], b_send, b_recv.at[g], geometries[AXES[g]]["dev_b"])

    def x_exchange(g):
        geo = geometries[AXES[g]]
        wait_for(br.at[g], b_recv.at[g])

        def add(i, _):
            rows = pl.ds(pl.multiple_of(i * 64, 64), 64)
            z32[g, rows, :] = quarter_sum(g, geo["quarter"], i) + br[g, rows, :].astype(F32)
            return 0

        lax.fori_loop(0, ZP // 64, add, 0)
        for i in range(8):
            xs[g, i] = z32[g, i * XP:(i + 1) * XP, :].astype(BF)
        for d in range(1, 8):
            send(xs.at[g, geo["peer"](d)], xr.at[g, d - 1], xy_send, xy_recv.at[g], geo["peer_dev"](d))

    def finish(g):
        geo = geometries[AXES[g]]
        wait_for(xr.at[g], xy_recv.at[g])
        total = z32[g, pl.ds(pl.multiple_of(geo["place"] * XP, 8), XP), :]
        for d in range(7):
            total = total + xr[g, d].astype(F32)
        fin[g, core, geo["quarter"] * 8 + geo["place"]] = (total * SCALE).astype(BF)
        piece = fin.at[g, core, geo["quarter"] * 8 + geo["place"]]
        for d in range(1, 8):
            send(piece, piece, gx_send, gx_recv.at[g], geo["peer_dev"](d))

    def gather_b(g):
        geo = geometries[AXES[g]]
        wait_for(xr.at[g], gx_recv.at[g])
        piece = fin.at[g, core, pl.ds(geo["quarter"] * 8, 8)]
        send(piece, piece, gb_send, gb_recv.at[g], geo["dev_b"])

    def gather_a(g):
        geo = geometries[AXES[g]]
        wait_for(fin.at[g, core, pl.ds(0, 8)], gb_recv.at[g])
        piece = fin.at[g, core, pl.ds(geo["half"] * 16, 16)]
        send(piece, piece, ga_send, ga_recv.at[g], geo["dev_a"])

    def gather_core(g):
        wait_for(fin.at[g, core, pl.ds(0, 16)], ga_recv.at[g])
        piece = fin.at[g, core]
        send(piece, piece, gc_send, gc_recv.at[g], twin)

    def write_out(g):
        wait_for(fin.at[g, 1 - core], gc_recv.at[g])
        for h in range(2):
            if g == 0:
                for k in range(3):
                    pltpu.make_async_copy(
                        fin.at[0, h, :, pl.ds(k * XS, XS), :],
                        gp_h.at[:, :, pl.ds(k * FW + h * 128, 128)], wout_sem,
                    ).start()
            else:
                pltpu.make_async_copy(
                    fin.at[g, h], gc_h.at[:, :, pl.ds((g - 1) * FW + h * 128, 128)], wout_sem
                ).start()

    def gelu(i):
        def tile(j, _):
            rows = pl.ds(pl.multiple_of(i * RB + j * 128, 128), 128)

            def strip(m, _):
                sub = pl.ds(pl.multiple_of(i * RB + j * 128 + m * 16, 16), 16)
                wide = io[sub, :].astype(F32)
                cumul = 0.5 * (1.0 + lax.erf(wide * (1.0 / math.sqrt(2.0))))
                dense = jnp.exp(-0.5 * wide * wide) * (1.0 / math.sqrt(2.0 * math.pi))
                der[sub, :] = cumul + wide * dense
                io[sub, :] = (wide * cumul).astype(BF)
                return 0

            lax.fori_loop(0, 8, strip, 0)
            h_t[:, rows] = io[rows, :].T
            return 0

        lax.fori_loop(0, RB // 128, tile, 0)

    tap_q = 2 * yh
    tap_x = 2 - 2 * yh

    def weight_tap(f, tap, taps):
        def tile(i, _):
            rows = pl.ds(pl.multiple_of(i * 256, 256), 256)
            value = dot(h_t[rows, :], taps[f])
            spot = pl.ds(pl.multiple_of(tap * CH + i * 256, 256), 256)
            slab[0, spot, :] = value[:, :128]
            slab[1, spot, :] = value[:, 128:]
            return 0

        lax.fori_loop(0, CH // 256, tile, 0)

    def data_rows(f, first, count):
        def tile(i, _):
            rows = pl.ds(pl.multiple_of(i * RB, RB), RB)
            total = dot_t(mid[f, rows, :], cw[f, 1])
            total = total + dot_t(mid_q[f, rows, :], cw[f, tap_q])
            total = total + dot_t(mid_x[f, rows, :], cw[f, tap_x])
            gh[rows, :] = total if f == 0 else gh[rows, :] + total
            if f == NF - 1:
                def strip(m, _):
                    sub = pl.ds(pl.multiple_of(i * RB + m * 16, 16), 16)
                    io[sub, :] = (cot[sub, :].astype(F32) + gh[sub, :] * der[sub, :]).astype(BF)
                    return 0

                lax.fori_loop(0, RB // 16, strip, 0)
                pltpu.make_async_copy(io.at[rows], gi_h.at[rows], out_sem).start()
            return 0

        lax.fori_loop(first, first + count, tile, 0)

    def x_tap(f):
        @pl.when(has_src)
        def _():
            wait_for(mid_x.at[f], x_recv.at[f])

        weight_tap(f, tap_x, mid_x)

    def prepare():
        ld_cout.wait()
        turn_rows()
        ld_inp.start()
        clear_x()

    def load_done():
        ld_inp.wait()
        for cp in ld_cw:
            cp.wait()

    stages = (
        core_send, core_sum, a_exchange, b_exchange, x_exchange, finish, gather_b, gather_a, gather_core, write_out
    )
    plan = {}

    def at(tick, action, *args):
        plan.setdefault(tick, []).append((action, args))

    at(0, part_chunk, 1, 0)
    at(1, prepare)
    at(2, proj_block, 0)
    at(2, proj_block, 1)
    at(3, proj_block, 2)
    at(4, part_chunk, 2, 0)
    at(5, load_done)
    for i in range(NB):
        at((5, 5, 6, 6, 6, 7, 7, 7)[i], gelu, i)
    for f in range(NF):
        base = NB * (f + 1)
        at(base, weight_tap, f, 1, mid)
        at(base + 1, weight_tap, f, tap_q, mid_q)
        at(base + X_TICK if f < NF - 1 else base + 3, x_tap, f)
    for g in (3, 0, 1, 2):
        for n, tick in enumerate(TICKS[g]):
            at(tick, stages[n], g)
    for f in range(NF):
        for i in range(4):
            at((NB * (f + 1) + X_TICK if f < NF - 1 else 28) + i, data_rows, f, 2 * i, 2)
    for tick in range(max(NT + LAG - 1, max(plan)) + 1):
        if tick < NT:
            service(tick)
        if LAG <= tick < NT + LAG:
            forward_x(tick - LAG)
        for action, args in plan.get(tick, ()):
            action(*args)

    wait_for(part, e_send)
    wait_for(mid, q_send)

    @pl.when(has_dst)
    def _():
        wait_for(mid_q, x_send)

    wait_for(cs, c_send)
    wait_for(as_, a_send)
    wait_for(bs, b_send)
    wait_for(xr, xy_send)
    wait_for(xr, gx_send)
    for g in range(NF + 1):
        wait_for(fin.at[g, 0, pl.ds(0, 8)], gb_send)
        wait_for(fin.at[g, 0, pl.ds(0, 16)], ga_send)
        wait_for(fin.at[g, 0], gc_send)
    wait_for(io, out_sem)
    wait_for(fin, wout_sem)


def shards(inputs, cotangent, conv_out, conv_weight, proj_weight):
    any_spec = pl.BlockSpec(memory_space=pl.ANY)
    dma = pltpu.SemaphoreType.DMA
    slabs = NF + 1
    rows_bf = pltpu.VMEM((ROWS, CH), BF)
    chunks = pltpu.VMEM((NF, ROWS, FW), BF)
    flat = [a.reshape(ROWS, CH) for a in (inputs, cotangent, conv_out)]
    grad_inputs, grad_conv, grad_proj = pl.pallas_call(
        kernel,
        out_shape=(
            jax.ShapeDtypeStruct((ROWS, CH), BF),
            jax.ShapeDtypeStruct((32, XP, FULL), BF),
            jax.ShapeDtypeStruct((32, XS, CH), BF),
        ),
        in_specs=[any_spec] * 5,
        out_specs=(any_spec,) * 3,
        scratch_shapes=[
            rows_bf, rows_bf, pltpu.VMEM((CH, ROWS), BF), pltpu.VMEM((ROWS, CH), F32),
            pltpu.VMEM((FULL, CH), BF), pltpu.VMEM((NF, 3, CH, FW), BF),
            chunks, chunks, chunks, chunks, pltpu.VMEM((ROWS, CH), F32),
            pltpu.VMEM((2, SLAB, 128), F32), pltpu.VMEM((slabs, ZH, 128), F32), pltpu.VMEM((slabs, ZP, 128), F32),
            pltpu.VMEM((slabs, SLAB, 128), BF), pltpu.VMEM((slabs, SLAB, 128), BF),
            pltpu.VMEM((slabs, ZH, 128), BF), pltpu.VMEM((slabs, ZH, 128), BF),
            pltpu.VMEM((slabs, ZP, 128), BF), pltpu.VMEM((slabs, ZP, 128), BF),
            pltpu.VMEM((slabs, 8, XP, 128), BF), pltpu.VMEM((slabs, 7, XP, 128), BF),
            pltpu.VMEM((slabs, 2, 32, XP, 128), BF),
            dma((4 + NF,)), dma, dma,
            dma, dma((NT,)), dma, dma((NT,)), dma, dma((NF,)),
        ] + [dma, dma((slabs,))] * 8,
        compiler_params=pltpu.CompilerParams(
            collective_id=0, has_side_effects=True, vmem_limit_bytes=62 * 1024 * 1024
        ),
    )(*flat, conv_weight, proj_weight)
    grad_conv = grad_conv.reshape(3, CH, FULL)
    grad_proj = grad_proj.reshape(FULL, CH)
    return (grad_inputs.reshape(inputs.shape), grad_conv, grad_proj)


def solution(mesh):
    in_specs = (
        P(None, "seq", "ch"),
        P(None, "seq", "ch"),
        P(None, "seq", None),
        P(None, "ch", None),
        P(None, "ch"),
    )
    out_specs = (P(None, "seq", "ch"), P(None, "ch", None), P(None, "ch"))
    return jax.shard_map(shards, mesh=mesh, in_specs=in_specs, out_specs=out_specs, check_vma=False)
```
